32 devices in a mesh: rows: 16 (over z, y, core), maze: 2 (over x).
Axes of the slice: x: 2, y: 2, z: 4, core: 2. Of those that a mesh axis runs over, the one named last changes fastest.
Arguments:
- maze_walls: int32 [2, 128, 256], P('maze', 'rows'), may hold values 0 or 1
- goal_cell: int32 [2, 2], P('maze'), may hold values from 0 to 127
- start_hidden: bfloat16 [2, 32, 128, 256], P('maze', None, 'rows'), may hold values from -0.8984375 to 0.8984375
- start_cell: float32 [2, 32, 128, 256], P('maze', None, 'rows'), may hold values from -4 to 4
- cotangent: bfloat16 [2, 3, 32, 128, 256], P('maze', None, None, 'rows'), may hold values from -6 to 6
- gate_weights: bfloat16 [73728], P(('rows', 'maze')), may hold values from -0.25 to 0.25
- embed_table: float32 [3, 32], replicated, may hold values from -4 to 4
Outputs:
- grad_weights: float32 [73728], P(('rows', 'maze'))
- grad_table: float32 [3, 32], replicated
- grad_hidden: float32 [2, 32, 128, 256], P('maze', None, 'rows')
- grad_cell: float32 [2, 32, 128, 256], P('maze', None, 'rows')
The draws below stay inside these ranges and needn't reach their ends.
Inputs may be any that keep to these rules, and one draw needn't show every extreme that they name: `maze_walls`: 0 for open cells, 1 for walls. `goal_cell`: goal row and column inside the grid.
All inputs are finite; a program needn't handle non-finite values. No bound on the sum of `maze_walls` on one device may be relied on, other than what follows from the above.
Results may differ from the reference program's by a relative error of at most 0.0044.
Values may be sent and summed in bfloat16 or wider, within the bound.
A program may use at most 64 MiB of HBM per device.

```python
import math
import jax
import jax.numpy as jnp
from jax import lax

XIN = 32
HID = 32
GATES = 128
STEPS = 3
COLS = 256
GRID_ROWS = 128
MAZES = 2


def plant(result, key, least, top_value):
    shape = result.shape
    index_at = [jax.random.randint(jax.random.fold_in(key, axis), (), 0, shape[axis]) for axis in range(len(shape))]
    result = result.at[tuple(index_at)].set(least)
    longest = shape.index(max(shape))
    index_at[longest] = (index_at[longest] + 1) % shape[longest]
    return result.at[tuple(index_at)].set(top_value)


def levels(stream_key, extent, split, low, high):
    loudness = 1.0
    for axis_at, parts in split:
        heights = jax.random.uniform(jax.random.fold_in(jax.random.fold_in(stream_key, 6), axis_at), (parts,), jnp.float32, low / len(split), high / len(split))
        loudness = loudness * jnp.repeat(jnp.exp(heights), extent[axis_at] // parts).reshape((-1,) + (1,) * (len(extent) - 1 - axis_at))
    return loudness


def bell_draw(key, extent, scale, most, cuts=(), kind=jnp.bfloat16):
    factor_of = levels(key, extent, cuts, -0.22, 0.18) if cuts else 1.0
    result = jax.random.normal(key, extent, jnp.float32) * scale * factor_of
    return jnp.minimum(jnp.maximum(result, -most), most).astype(kind)


def setup_inputs(seed: int = 0) -> dict:
    seeds = jax.random.split(jax.random.key(seed), 8)
    return {
        "maze_walls": plant((jax.random.randint(seeds[0], (MAZES, GRID_ROWS, COLS), 0, 3) < 1).astype(jnp.int32), jax.random.fold_in(seeds[0], 1), 0, 1),
        "goal_cell": plant(jax.random.randint(seeds[1], (MAZES, 2), 0, min(GRID_ROWS, COLS)), jax.random.fold_in(seeds[1], 1), 0, (min(GRID_ROWS, COLS)) - 1).astype(jnp.int32),
        "start_hidden": jnp.clip(jax.random.uniform(seeds[2], (MAZES, HID, GRID_ROWS, COLS), jnp.float32, -0.8984375, 0.8984375) * levels(seeds[2], (MAZES, HID, GRID_ROWS, COLS), ((0, 2), (2, 16)), -0.4, 0.0), -0.8984375, 0.8984375).astype(jnp.bfloat16),
        "start_cell": bell_draw(seeds[3], (MAZES, HID, GRID_ROWS, COLS), 1.0, 4.0, ((0, 2), (2, 16)), jnp.float32),
        "cotangent": bell_draw(seeds[4], (MAZES, STEPS, HID, GRID_ROWS, COLS), 1.0, 6.0, ((0, 2), (3, 16))),
        "gate_weights": bell_draw(seeds[5], (9 * GATES * (XIN + HID),), (9 * (XIN + HID)) ** -0.5, 0.25, ((0, 32),)),
        "embed_table": bell_draw(seeds[6], (3, XIN), 1.0, 4.0, (), jnp.float32),
    }


goal_reach = 64.0

def tap_offsets():
    return [(row_off, col_off) for row_off in (-1, 0, 1) for col_off in (-1, 0, 1)]

def gate_conv(padded, kernel, row_count, col_count):
    summed = None
    for tap_index, (row_off, col_off) in enumerate(tap_offsets()):
        window = padded[:, 1 + row_off:1 + row_off + row_count, 1 + col_off:1 + col_off + col_count]
        tap_term = jnp.einsum('gc,crq->grq', kernel[tap_index], window)
        summed = tap_term if summed is None else summed + tap_term
    return summed

def input_grads(grad_padded, kernel, row_count, col_count):
    summed = None
    for tap_index, (row_off, col_off) in enumerate(tap_offsets()):
        window = grad_padded[:, 1 - row_off:1 - row_off + row_count, 1 - col_off:1 - col_off + col_count]
        tap_term = jnp.einsum('gc,grq->crq', kernel[tap_index], window)
        summed = tap_term if summed is None else summed + tap_term
    return summed

def weight_grads(gate_grad, padded, row_count, col_count):
    pieces = []
    for row_off, col_off in tap_offsets():
        window = padded[:, 1 + row_off:1 + row_off + row_count, 1 + col_off:1 + col_off + col_count]
        pieces.append(jnp.einsum('grq,crq->gc', gate_grad, window))
    return jnp.stack(pieces)

def one_maze(maze_walls, goal_cell, start_hidden, start_cell, cotangent, kernel, embed_table):
    row_count, col_count = maze_walls.shape
    wall_mask = (maze_walls == 1).astype(jnp.float32)
    row_pos = jnp.arange(row_count, dtype=jnp.int32)[:, None]
    col_pos = jnp.arange(col_count, dtype=jnp.int32)[None, :]
    distance = (jnp.abs(row_pos - goal_cell[0]) + jnp.abs(col_pos - goal_cell[1])).astype(jnp.float32)
    goal_bump = jnp.exp(-distance / goal_reach)
    inputs = (embed_table[0][:, None, None] * (1.0 - wall_mask) + embed_table[1][:, None, None] * wall_mask + embed_table[2][:, None, None] * goal_bump).astype(jnp.bfloat16)
    inputs = lax.optimization_barrier(inputs)
    hidden = start_hidden
    cell_state = start_cell.astype(jnp.float32)
    stored = []
    for step_index in range(STEPS):
        stacked = jnp.concatenate([inputs, hidden], axis=0).astype(jnp.float32)
        padded = jnp.pad(stacked, ((0, 0), (1, 1), (1, 1)))
        pre_gate = gate_conv(padded, kernel, row_count, col_count)
        in_gate = jax.nn.sigmoid(pre_gate[:HID])
        forget_gate = jax.nn.sigmoid(pre_gate[HID:2 * HID] + 1.0)
        out_gate = jax.nn.sigmoid(pre_gate[2 * HID:3 * HID])
        cand_gate = jnp.tanh(pre_gate[3 * HID:])
        new_cell = forget_gate * cell_state + in_gate * cand_gate
        squash = jnp.tanh(new_cell)
        stored.append((padded, cell_state, in_gate, forget_gate, out_gate, cand_gate, squash))
        hidden = lax.optimization_barrier((out_gate * squash).astype(jnp.bfloat16))
        cell_state = new_cell
    carry_hidden = jnp.zeros((HID, row_count, col_count), jnp.float32)
    carry_cell = jnp.zeros((HID, row_count, col_count), jnp.float32)
    kernel_acc = jnp.zeros((9, GATES, XIN + HID), jnp.float32)
    input_acc = jnp.zeros((XIN, row_count, col_count), jnp.float32)
    for step_index in reversed(range(STEPS)):
        padded, prev_cell, in_gate, forget_gate, out_gate, cand_gate, squash = stored[step_index]
        hid_grad = cotangent[step_index].astype(jnp.float32) + carry_hidden
        cell_grad = carry_cell + hid_grad * out_gate * (1.0 - squash * squash)
        gate_grad = jnp.concatenate([cell_grad * cand_gate * in_gate * (1.0 - in_gate), cell_grad * prev_cell * forget_gate * (1.0 - forget_gate), hid_grad * squash * out_gate * (1.0 - out_gate), cell_grad * in_gate * (1.0 - cand_gate * cand_gate)], axis=0).astype(jnp.bfloat16)
        gate_grad = lax.optimization_barrier(gate_grad).astype(jnp.float32)
        kernel_acc = kernel_acc + weight_grads(gate_grad, padded, row_count, col_count)
        grad_padded = jnp.pad(gate_grad, ((0, 0), (1, 1), (1, 1)))
        stack_grad = input_grads(grad_padded, kernel, row_count, col_count)
        input_acc = input_acc + stack_grad[:XIN]
        carry_hidden = stack_grad[XIN:]
        carry_cell = cell_grad * forget_gate
    table_part = jnp.stack([lax.optimization_barrier(jnp.sum(input_acc * (1.0 - wall_mask), axis=(1, 2))), lax.optimization_barrier(jnp.sum(input_acc * wall_mask, axis=(1, 2))), lax.optimization_barrier(jnp.sum(input_acc * goal_bump, axis=(1, 2)))])
    return (kernel_acc, table_part, carry_hidden, carry_cell)

def reference(maze_walls, goal_cell, start_hidden, start_cell, cotangent, gate_weights, embed_table):
    kernel = gate_weights.astype(jnp.float32).reshape(9, GATES, XIN + HID)

    def per_maze(items):
        return one_maze(items[0], items[1], items[2], items[3], items[4], kernel, embed_table)
    kernel_all, table_all, grad_hidden, grad_cell = lax.map(per_maze, (maze_walls, goal_cell, start_hidden, start_cell, cotangent))
    scale = 1.0 / math.sqrt(MAZES * GRID_ROWS * COLS * STEPS)
    grad_weights = (lax.optimization_barrier(jnp.sum(kernel_all, axis=0)) * scale).reshape(-1)
    grad_table = lax.optimization_barrier(jnp.sum(table_all, axis=0)) * scale
    return (grad_weights, grad_table, grad_hidden, grad_cell)
```

```python
import functools
import math

import jax
import jax.numpy as jnp
from jax import lax
from jax.experimental import pallas as pl
from jax.experimental.pallas import tpu as pltpu
from jax.sharding import PartitionSpec as P

goal_reach = 64.0
MESH = pl.DeviceIdType.MESH
VMEM = pl.BlockSpec(memory_space=pltpu.VMEM)
SMEM = pl.BlockSpec(memory_space=pltpu.SMEM)
direct_limit = 64


def flat_peer(index, mazes):
    return {"rows": lax.div(index, mazes), "maze": lax.rem(index, mazes)}


def flat_self(mazes):
    return lax.axis_index("rows") * mazes + lax.axis_index("maze")


def greet_all(count, mazes):
    me = flat_self(mazes)
    barrier = pltpu.get_barrier_semaphore()

    def greet(step, _):
        peer = lax.rem(me + step, count)
        pl.semaphore_signal(
            barrier, inc=1, device_id=flat_peer(peer, mazes), device_id_type=MESH
        )
        return 0

    lax.fori_loop(1, count, greet, 0)
    pl.semaphore_wait(barrier, count - 1)


def gather_kernel(count, mazes, shard_ref, out_ref, send_sem, recv_sem):
    me = flat_self(mazes)
    greet_all(count, mazes)

    def push(step):
        return pltpu.make_async_remote_copy(
            src_ref=shard_ref,
            dst_ref=out_ref.at[me],
            send_sem=send_sem.at[step],
            recv_sem=recv_sem.at[step],
            device_id=flat_peer(lax.rem(me + step, count), mazes),
            device_id_type=MESH,
        )

    def start(step, _):
        push(step).start()
        return 0

    def finish(step, _):
        push(step).wait()
        return 0

    lax.fori_loop(1, count, start, 0)
    out_ref[me] = shard_ref[...]
    lax.fori_loop(1, count, finish, 0)


def gather_weights(shard, count, mazes):
    size = shard.shape[0]
    if size % 128 or count > direct_limit:
        return lax.all_gather(shard, ("rows", "maze"), axis=0, tiled=True)
    height = size // 128
    out = pl.pallas_call(
        functools.partial(gather_kernel, count, mazes),
        out_shape=jax.ShapeDtypeStruct((count, height, 128), shard.dtype),
        in_specs=[VMEM],
        out_specs=VMEM,
        scratch_shapes=[
            pltpu.SemaphoreType.DMA((count,)),
            pltpu.SemaphoreType.DMA((count,)),
        ],
        compiler_params=pltpu.CompilerParams(collective_id=0, has_side_effects=True),
    )(shard.reshape(height, 128))
    return out.reshape(-1)


def scatter_kernel(
    count, mazes, height, scale, chunk_ref, weight_ref, table_ref, landed, send_sem, recv_sem
):
    me = flat_self(mazes)
    greet_all(count, mazes)

    def push(step):
        peer = lax.rem(me + step, count)
        return pltpu.make_async_remote_copy(
            src_ref=chunk_ref.at[peer],
            dst_ref=landed.at[me],
            send_sem=send_sem.at[step],
            recv_sem=recv_sem.at[step],
            device_id=flat_peer(peer, mazes),
            device_id_type=MESH,
        )

    def start(step, _):
        push(step).start()
        return 0

    def finish(step, _):
        push(step).wait()
        return 0

    lax.fori_loop(1, count, start, 0)
    landed[me] = chunk_ref[me]
    lax.fori_loop(1, count, finish, 0)
    total = landed[0]
    for slot in range(1, count):
        total = total + landed[slot]
    total = total * scale
    weight_ref[...] = total[:height]
    table_ref[...] = total[height : height + 3, : table_ref.shape[1]]


def scatter_grads(chunks, height, input_width, scale, count, mazes):
    return pl.pallas_call(
        functools.partial(scatter_kernel, count, mazes, height, scale),
        out_shape=(
            jax.ShapeDtypeStruct((height, 128), jnp.float32),
            jax.ShapeDtypeStruct((3, input_width), jnp.float32),
        ),
        in_specs=[VMEM],
        out_specs=(VMEM, VMEM),
        scratch_shapes=[
            pltpu.VMEM(chunks.shape, jnp.float32),
            pltpu.SemaphoreType.DMA((count,)),
            pltpu.SemaphoreType.DMA((count,)),
        ],
        compiler_params=pltpu.CompilerParams(collective_id=2, has_side_effects=True),
    )(chunks)


def logistic(x):
    return 0.5 * jnp.tanh(0.5 * x) + 0.5


def main_kernel(
    chunk_rows,
    goal_ref,
    walls_ref,
    embed_ref,
    hidden_ref,
    cell_ref,
    cot_ref,
    forward_ref,
    backward_ref,
    kernel_ref,
    table_ref,
    carry_h_ref,
    carry_c_ref,
    fields,
    grads,
    cells,
    acts,
    squashes,
    input_acc,
    kernel_acc,
    field_land,
    grad_land,
    field_send,
    field_recv,
    grad_send,
    grad_recv,
):
    row_count, width, col_count = hidden_ref.shape
    in_width = embed_ref.shape[0]
    channels = in_width + width
    gates = 4 * width
    steps = cot_ref.shape[0]
    me = lax.axis_index("rows")
    ends = lax.axis_size("rows") - 1
    lane = lax.broadcasted_iota(jnp.int32, (1, col_count), 1)
    has_left = (lane > 0).astype(jnp.float32)
    has_right = (lane < col_count - 1).astype(jnp.float32)

    barrier = pltpu.get_barrier_semaphore()

    @pl.when(me > 0)
    def _():
        pl.semaphore_signal(barrier, inc=1, device_id={"rows": me - 1}, device_id_type=MESH)

    @pl.when(me < ends)
    def _():
        pl.semaphore_signal(barrier, inc=1, device_id={"rows": me + 1}, device_id_type=MESH)

    def masks(row):
        wall = (walls_ref[pl.ds(row, 1), :] == 1).astype(jnp.float32)
        row_dist = jnp.abs(me * row_count + row - goal_ref[0, 0])
        dist = (row_dist + jnp.abs(lane - goal_ref[0, 1])).astype(jnp.float32)
        return 1.0 - wall, wall, jnp.exp(-dist / goal_reach)

    def set_field(step, row, low, values):
        high = low + values.shape[0]
        wide = values.astype(jnp.float32)
        fields[step, row, low:high] = (pltpu.roll(wide, 1, 1) * has_left).astype(jnp.bfloat16)
        fields[step, row, channels + low : channels + high] = values
        fields[step, row, 2 * channels + low : 2 * channels + high] = (
            pltpu.roll(wide, col_count - 1, 1) * has_right
        ).astype(jnp.bfloat16)

    def share_inputs(step, row):
        for tap in range(3):
            part = slice(tap * channels, tap * channels + in_width)
            fields[step, row, part] = fields[0, row, part]

    def first_row(row, _):
        open_mask, wall_mask, bump = masks(row)
        values = (
            embed_ref[:, 0:1] * open_mask + embed_ref[:, 1:2] * wall_mask + embed_ref[:, 2:3] * bump
        ).astype(jnp.bfloat16)
        set_field(0, row + 1, 0, values)
        set_field(0, row + 1, in_width, hidden_ref[row])
        for step in range(1, steps):
            share_inputs(step, row + 1)
        cells[0, row] = cell_ref[row]
        return 0

    lax.fori_loop(0, row_count, first_row, 0)

    middle = jnp.logical_and(me > 0, me < ends)

    @pl.when(middle)
    def _():
        pl.semaphore_wait(barrier, 2)

    @pl.when(jnp.logical_not(middle))
    def _():
        pl.semaphore_wait(barrier, 1)

    def field_copy(step, side):
        low = channels if step == 0 else channels + in_width
        size = 2 * channels - low
        row = 1 if side == 0 else row_count
        return pltpu.make_async_remote_copy(
            src_ref=fields.at[step, row, pl.ds(low, size)],
            dst_ref=field_land.at[step, 1 - side, pl.ds(low - channels, size)],
            send_sem=field_send.at[step, side],
            recv_sem=field_recv.at[step, 1 - side],
            device_id={"rows": me - 1 if side == 0 else me + 1},
            device_id_type=MESH,
        )

    def grad_copy(step, side):
        row = 1 if side == 0 else row_count
        return pltpu.make_async_remote_copy(
            src_ref=grads.at[step, row],
            dst_ref=grad_land.at[step, 1 - side],
            send_sem=grad_send.at[step, side],
            recv_sem=grad_recv.at[step, 1 - side],
            device_id={"rows": me - 1 if side == 0 else me + 1},
            device_id_type=MESH,
        )

    def send_both(copy, step):
        @pl.when(me > 0)
        def _():
            copy(step, 0).start()

        @pl.when(me < ends)
        def _():
            copy(step, 1).start()

    def take_fields(step):
        low = 0 if step == 0 else in_width
        for side, row, there in ((0, 0, me > 0), (1, row_count + 1, me < ends)):

            @pl.when(there)
            def _():
                field_copy(step, side).wait_send()
                field_copy(step, 1 - side).wait_recv()
                if step:
                    share_inputs(step, row)
                set_field(step, row, low, field_land[step, side, low:channels])

            @pl.when(jnp.logical_not(there))
            def _():
                fields[step, row] = jnp.zeros((3 * channels, col_count), jnp.bfloat16)

    def take_grads(step):
        for side, row, there in ((0, 0, me > 0), (1, row_count + 1, me < ends)):

            @pl.when(there)
            def _():
                grad_copy(step, side).wait_send()
                grad_copy(step, 1 - side).wait_recv()
                grads[step, row] = grad_land[step, side]

            @pl.when(jnp.logical_not(there))
            def _():
                grads[step, row] = jnp.zeros((gates, col_count), jnp.bfloat16)

    def window(step, row):
        return fields[step, pl.ds(row, 3)].reshape(9 * channels, col_count)

    def forward_row(step, row):
        pre = jnp.dot(forward_ref[...], window(step, row), preferred_element_type=jnp.float32)
        in_gate = logistic(pre[:width])
        forget_gate = logistic(pre[width : 2 * width] + 1.0)
        out_gate = logistic(pre[2 * width : 3 * width])
        cand = jnp.tanh(pre[3 * width :])
        new_cell = forget_gate * cells[step, row] + in_gate * cand
        squash = jnp.tanh(new_cell)
        acts[step, row, :width] = in_gate
        acts[step, row, width : 2 * width] = forget_gate
        acts[step, row, 2 * width : 3 * width] = out_gate
        acts[step, row, 3 * width :] = cand
        squashes[step, row] = squash
        if step < steps - 1:
            cells[step + 1, row] = new_cell
            set_field(step + 1, row + 1, in_width, (out_gate * squash).astype(jnp.bfloat16))

    def for_rows(low, high, body):
        def run(row, _):
            body(row)
            return 0

        lax.fori_loop(low, high, run, 0)

    for step in range(steps):
        send_both(field_copy, step)
        for_rows(1, row_count - 1, functools.partial(forward_row, step))
        take_fields(step)
        forward_row(step, 0)
        forward_row(step, row_count - 1)

    def gate_row(step, row):
        in_gate = acts[step, row, :width]
        forget_gate = acts[step, row, width : 2 * width]
        out_gate = acts[step, row, 2 * width : 3 * width]
        cand = acts[step, row, 3 * width :]
        squash = squashes[step, row]
        hid_grad = cot_ref[step, row].astype(jnp.float32)
        if step < steps - 1:
            hid_grad = hid_grad + carry_h_ref[row]
        cell_grad = hid_grad * out_gate * (1.0 - squash * squash)
        if step < steps - 1:
            cell_grad = cell_grad + carry_c_ref[row]
        parts = (
            cell_grad * cand * in_gate * (1.0 - in_gate),
            cell_grad * cells[step, row] * forget_gate * (1.0 - forget_gate),
            hid_grad * squash * out_gate * (1.0 - out_gate),
            cell_grad * in_gate * (1.0 - cand * cand),
        )
        for index, part in enumerate(parts):
            grads[step, row + 1, index * width : (index + 1) * width] = part.astype(jnp.bfloat16)
        carry_c_ref[row] = cell_grad * forget_gate

    def back_row(step, row):
        stack = grads[step, pl.ds(row, 3)].reshape(3 * gates, col_count)
        out = jnp.dot(backward_ref[...], stack, preferred_element_type=jnp.float32)
        summed = (
            pltpu.roll(out[:channels], col_count - 1, 1) * has_right
            + out[channels : 2 * channels]
            + pltpu.roll(out[2 * channels :], 1, 1) * has_left
        )
        if step < steps - 1:
            input_acc[row] = input_acc[row] + summed[:in_width]
        else:
            input_acc[row] = summed[:in_width]
        carry_h_ref[row] = summed[in_width:]

    def kernel_rows(step, row):
        total = None
        for part in range(2):
            term = lax.dot_general(
                grads[step, row + part + 1],
                window(step, row + part),
                (((1,), (1,)), ((), ())),
                preferred_element_type=jnp.float32,
            )
            total = term if total is None else total + term
        for block in range(kernel_acc.shape[0]):
            part = total[:, block * 128 : (block + 1) * 128]
            lanes = part.shape[1]
            kernel_acc[block, :, :lanes] = kernel_acc[block, :, :lanes] + part

    kernel_acc[...] = jnp.zeros(kernel_acc.shape, jnp.float32)
    for step in reversed(range(steps)):
        gate_row(step, 0)
        gate_row(step, row_count - 1)
        send_both(grad_copy, step)
        for_rows(1, row_count - 1, functools.partial(gate_row, step))
        for_rows(1, row_count - 1, functools.partial(back_row, step))
        for_rows(0, row_count // 2, lambda pair: kernel_rows(step, 2 * pair))
        take_grads(step)
        back_row(step, 0)
        back_row(step, row_count - 1)

    def table_row(row, sums):
        grad = input_acc[row]
        return tuple(total + grad * mask for total, mask in zip(sums, masks(row)))

    zero = jnp.zeros((in_width, col_count), jnp.float32)
    sums = lax.fori_loop(0, row_count, table_row, (zero, zero, zero))
    columns = lax.broadcasted_iota(jnp.int32, (128, 128), 1)
    table = jnp.zeros((128, 128), jnp.float32)
    for index, total in enumerate(sums):
        column = jnp.sum(total, axis=1, keepdims=True)
        column = jnp.concatenate([column, jnp.zeros((128 - in_width, 1), jnp.float32)], axis=0)
        table = jnp.where(columns == index, column, table)
    flipped = table.T

    if chunk_rows:
        half = columns[: gates // 2] < channels
        lines = []
        for pair in range(5):
            even = kernel_acc[pair, pl.ds(0, gates // 2, stride=2), :]
            odd = kernel_acc[pair, pl.ds(1, gates // 2, stride=2), :]
            lines.append(jnp.where(half, even, pltpu.roll(odd, 64, 1)))
            if pair < 4:
                lines.append(jnp.where(half, pltpu.roll(even, 64, 1), odd))
        flat = jnp.concatenate(lines, axis=0)
        for index in range(kernel_ref.shape[0]):
            kernel_ref[index, :chunk_rows] = flat[index * chunk_rows : (index + 1) * chunk_rows]
            kernel_ref[index, chunk_rows : chunk_rows + 3] = flipped[:3]
            rest = kernel_ref.shape[1] - chunk_rows - 3
            kernel_ref[index, chunk_rows + 3 :] = jnp.zeros((rest, 128), jnp.float32)
    else:
        for block in range(kernel_acc.shape[0]):
            lanes = min(128, 9 * channels - block * 128)
            kernel_ref[:, block * 128 : block * 128 + lanes] = kernel_acc[block, :, :lanes]
    table_ref[...] = flipped[:8]


def per_device(
    maze_walls, goal_cell, start_hidden, start_cell, cotangent, gate_weights, embed_table
):
    rows = lax.axis_size("rows")
    mazes = lax.axis_size("maze")
    count = rows * mazes
    row_count = maze_walls.shape[1]
    col_count = maze_walls.shape[2]
    width = start_hidden.shape[1]
    in_width = embed_table.shape[1]
    channels = in_width + width
    gates = 4 * width
    steps = cotangent.shape[1]
    size = gate_weights.shape[0]
    kernel = gather_weights(gate_weights, count, mazes).reshape(3, 3, gates, channels)
    forward = kernel.transpose(2, 0, 1, 3).reshape(gates, 9 * channels)
    backward = kernel[::-1].transpose(1, 3, 0, 2).reshape(3 * channels, 3 * gates)
    hidden = start_hidden[0].transpose(1, 0, 2)
    cell = start_cell[0].transpose(1, 0, 2)
    cot = cotangent[0].transpose(0, 2, 1, 3)
    scale = 1.0 / math.sqrt(count * row_count * col_count * steps)

    direct = size % 128 == 0 and count <= direct_limit and channels == 64
    chunk_rows = size // 128 if direct else 0
    if direct:
        kernel_shape = (count, -(-(chunk_rows + 3) // 8) * 8, 128)
    else:
        kernel_shape = (gates, 9 * channels)
    f32 = jnp.float32
    bf16 = jnp.bfloat16
    grad_kernel, table, carry_h, carry_c = pl.pallas_call(
        functools.partial(main_kernel, chunk_rows),
        out_shape=(
            jax.ShapeDtypeStruct(kernel_shape, f32),
            jax.ShapeDtypeStruct((8, 128), f32),
            jax.ShapeDtypeStruct((row_count, width, col_count), f32),
            jax.ShapeDtypeStruct((row_count, width, col_count), f32),
        ),
        in_specs=[SMEM] + [VMEM] * 7,
        out_specs=(VMEM, VMEM, VMEM, VMEM),
        scratch_shapes=[
            pltpu.VMEM((steps, row_count + 2, 3 * channels, col_count), bf16),
            pltpu.VMEM((steps, row_count + 2, gates, col_count), bf16),
            pltpu.VMEM((steps, row_count, width, col_count), f32),
            pltpu.VMEM((steps, row_count, gates, col_count), f32),
            pltpu.VMEM((steps, row_count, width, col_count), f32),
            pltpu.VMEM((row_count, in_width, col_count), f32),
            pltpu.VMEM((-(-9 * channels // 128), gates, 128), f32),
            pltpu.VMEM((steps, 2, channels, col_count), bf16),
            pltpu.VMEM((steps, 2, gates, col_count), bf16),
            pltpu.SemaphoreType.DMA((steps, 2)),
            pltpu.SemaphoreType.DMA((steps, 2)),
            pltpu.SemaphoreType.DMA((steps, 2)),
            pltpu.SemaphoreType.DMA((steps, 2)),
        ],
        compiler_params=pltpu.CompilerParams(
            collective_id=1, has_side_effects=True, vmem_limit_bytes=48 * 1024 * 1024
        ),
    )(
        goal_cell,
        maze_walls[0],
        embed_table.T,
        hidden,
        cell,
        cot,
        forward,
        backward,
    )
    if direct:
        grad_weights, grad_table = scatter_grads(
            grad_kernel, chunk_rows, in_width, scale, count, mazes
        )
        grad_weights = grad_weights.reshape(-1)
    else:
        ordered = grad_kernel.reshape(gates, 9, channels).transpose(1, 0, 2).reshape(-1)
        grad_weights = scale * lax.psum_scatter(
            ordered, ("rows", "maze"), scatter_dimension=0, tiled=True
        )
        grad_table = scale * lax.psum(table[:3, :in_width], ("rows", "maze"))
    return (
        grad_weights,
        grad_table,
        carry_h.transpose(1, 0, 2)[None],
        carry_c.transpose(1, 0, 2)[None],
    )


def solution(mesh):
    return jax.shard_map(
        per_device,
        mesh=mesh,
        in_specs=(
            P("maze", "rows", None),
            P("maze", None),
            P("maze", None, "rows", None),
            P("maze", None, "rows", None),
            P("maze", None, None, "rows", None),
            P(("rows", "maze")),
            P(),
        ),
        out_specs=(
            P(("rows", "maze")),
            P(),
            P("maze", None, "rows", None),
            P("maze", None, "rows", None),
        ),
        check_vma=False,
    )
```

```python
import functools
import math

import jax
import jax.numpy as jnp
from jax import lax
from jax.experimental import pallas as pl
from jax.experimental.pallas import tpu as pltpu
from jax.sharding import PartitionSpec as P

goal_reach = 64.0
MESH = pl.DeviceIdType.MESH
VMEM = pl.BlockSpec(memory_space=pltpu.VMEM)
SMEM = pl.BlockSpec(memory_space=pltpu.SMEM)


class Groups:
    def __init__(self, depth):
        rows = lax.axis_index("rows")
        self.depth = depth
        self.maze = lax.axis_index("maze")
        self.core = lax.rem(rows, 2)
        self.z = lax.div(rows, 4)
        self.y = lax.rem(lax.div(rows, 2), 2)
        self.plane = self.y * 2 + self.maze

    def device(self, z, plane, core):
        return {"rows": z * 4 + lax.div(plane, 2) * 2 + core, "maze": lax.rem(plane, 2)}

    def z_peer(self, step):
        z = lax.rem(self.z + step, self.depth)
        return z, self.device(z, self.plane, self.core)

    def plane_peer(self, step):
        plane = lax.rem(self.plane + step, 4)
        return plane, self.device(self.z, plane, self.core)

    def core_peer(self):
        return self.device(self.z, self.plane, 1 - self.core)

    def peers(self):
        found = [self.z_peer(step)[1] for step in range(1, self.depth)]
        found += [self.plane_peer(step)[1] for step in range(1, 4)]
        return found + [self.core_peer()]


def shard_slots(depth):
    return [
        (core, 2 * y + maze, z)
        for z in range(depth)
        for y in range(2)
        for core in range(2)
        for maze in range(2)
    ]


def push(src, dst, sems, slot, device):
    return pltpu.make_async_remote_copy(
        src_ref=src,
        dst_ref=dst,
        send_sem=sems.at[0, slot],
        recv_sem=sems.at[1, slot],
        device_id=device,
        device_id_type=MESH,
    )


def logistic(x):
    return 0.5 * jnp.tanh(0.5 * x) + 0.5


def main_kernel(
    depth,
    scale,
    goal_ref,
    walls_ref,
    embed_ref,
    hidden_ref,
    cell_ref,
    cot_ref,
    *refs,
):
    if depth:
        shard_ref, *refs = refs
    else:
        forward_ref, backward_ref, *refs = refs
    kernel_ref, table_ref, carry_h_ref, carry_c_ref, *refs = refs
    if depth:
        refs, extra = refs[:-14], refs[-14:]
        forward_ref, backward_ref, shards, chunks = extra[:4]
        core_land, plane_land, z_sum, z_land = extra[4:8]
        z_gather, plane_gather, core_gather = extra[8:11]
        core_scatter, plane_scatter, z_scatter = extra[11:]
    (
    fields,
    grads,
    cells,
    acts,
    squashes,
    input_acc,
    kernel_acc,
    field_land,
    grad_land,
    field_send,
    field_recv,
    grad_send,
    grad_recv,
    ) = refs
    row_count, width, col_count = hidden_ref.shape
    in_width = embed_ref.shape[0]
    channels = in_width + width
    gates = 4 * width
    steps = cot_ref.shape[0]
    me = lax.axis_index("rows")
    ends = lax.axis_size("rows") - 1
    lane = lax.broadcasted_iota(jnp.int32, (1, col_count), 1)
    has_left = (lane > 0).astype(jnp.float32)
    has_right = (lane < col_count - 1).astype(jnp.float32)

    barrier = pltpu.get_barrier_semaphore()

    @pl.when(me > 0)
    def _():
        pl.semaphore_signal(barrier, inc=1, device_id={"rows": me - 1}, device_id_type=MESH)

    @pl.when(me < ends)
    def _():
        pl.semaphore_signal(barrier, inc=1, device_id={"rows": me + 1}, device_id_type=MESH)

    group_peers = 0
    if depth:
        groups = Groups(depth)
        z_me, plane_me, core_me = groups.z, groups.plane, groups.core
        for peer in groups.peers():
            pl.semaphore_signal(barrier, inc=1, device_id=peer, device_id_type=MESH)
            group_peers += 1
        shards[core_me, plane_me, z_me] = shard_ref[...]
    middle = jnp.logical_and(me > 0, me < ends)

    @pl.when(middle)
    def _():
        pl.semaphore_wait(barrier, group_peers + 2)

    @pl.when(jnp.logical_not(middle))
    def _():
        pl.semaphore_wait(barrier, group_peers + 1)

    gathers = ([], [], [])
    if depth:
        for step in range(1, depth):
            part = shards.at[core_me, plane_me, z_me]
            gathers[0].append(push(part, part, z_gather, step, groups.z_peer(step)[1]))
        for step in range(1, 4):
            part = shards.at[core_me, plane_me]
            gathers[1].append(push(part, part, plane_gather, step, groups.plane_peer(step)[1]))
        part = shards.at[core_me]
        gathers[2].append(push(part, part, core_gather, 0, groups.core_peer()))
        for copy in gathers[0]:
            copy.start()

    def masks(row):
        wall = (walls_ref[pl.ds(row, 1), :] == 1).astype(jnp.float32)
        row_dist = jnp.abs(me * row_count + row - goal_ref[0, 0])
        dist = (row_dist + jnp.abs(lane - goal_ref[0, 1])).astype(jnp.float32)
        return 1.0 - wall, wall, jnp.exp(-dist / goal_reach)

    def set_field(step, row, low, values):
        high = low + values.shape[0]
        wide = values.astype(jnp.float32)
        fields[step, row, low:high] = (pltpu.roll(wide, 1, 1) * has_left).astype(jnp.bfloat16)
        fields[step, row, channels + low : channels + high] = values
        fields[step, row, 2 * channels + low : 2 * channels + high] = (
            pltpu.roll(wide, col_count - 1, 1) * has_right
        ).astype(jnp.bfloat16)

    def share_inputs(step, row):
        for tap in range(3):
            part = slice(tap * channels, tap * channels + in_width)
            fields[step, row, part] = fields[0, row, part]

    def first_row(row, _):
        open_mask, wall_mask, bump = masks(row)
        values = (
            embed_ref[:, 0:1] * open_mask + embed_ref[:, 1:2] * wall_mask + embed_ref[:, 2:3] * bump
        ).astype(jnp.bfloat16)
        set_field(0, row + 1, 0, values)
        set_field(0, row + 1, in_width, hidden_ref[row])
        for step in range(1, steps):
            share_inputs(step, row + 1)
        cells[0, row] = cell_ref[row]
        return 0

    lax.fori_loop(0, row_count, first_row, 0)


    def field_copy(step, side):
        low = channels if step == 0 else channels + in_width
        size = 2 * channels - low
        row = 1 if side == 0 else row_count
        return pltpu.make_async_remote_copy(
            src_ref=fields.at[step, row, pl.ds(low, size)],
            dst_ref=field_land.at[step, 1 - side, pl.ds(low - channels, size)],
            send_sem=field_send.at[step, side],
            recv_sem=field_recv.at[step, 1 - side],
            device_id={"rows": me - 1 if side == 0 else me + 1},
            device_id_type=MESH,
        )

    def grad_copy(step, side):
        row = 1 if side == 0 else row_count
        return pltpu.make_async_remote_copy(
            src_ref=grads.at[step, row],
            dst_ref=grad_land.at[step, 1 - side],
            send_sem=grad_send.at[step, side],
            recv_sem=grad_recv.at[step, 1 - side],
            device_id={"rows": me - 1 if side == 0 else me + 1},
            device_id_type=MESH,
        )

    def send_both(copy, step):
        @pl.when(me > 0)
        def _():
            copy(step, 0).start()

        @pl.when(me < ends)
        def _():
            copy(step, 1).start()

    def take_fields(step):
        low = 0 if step == 0 else in_width
        for side, row, there in ((0, 0, me > 0), (1, row_count + 1, me < ends)):

            @pl.when(there)
            def _():
                field_copy(step, side).wait_send()
                field_copy(step, 1 - side).wait_recv()
                if step:
                    share_inputs(step, row)
                set_field(step, row, low, field_land[step, side, low:channels])

            @pl.when(jnp.logical_not(there))
            def _():
                fields[step, row] = jnp.zeros((3 * channels, col_count), jnp.bfloat16)

    def take_grads(step):
        for side, row, there in ((0, 0, me > 0), (1, row_count + 1, me < ends)):

            @pl.when(there)
            def _():
                grad_copy(step, side).wait_send()
                grad_copy(step, 1 - side).wait_recv()
                grads[step, row] = grad_land[step, side]

            @pl.when(jnp.logical_not(there))
            def _():
                grads[step, row] = jnp.zeros((gates, col_count), jnp.bfloat16)

    def window(step, row):
        return fields[step, pl.ds(row, 3)].reshape(9 * channels, col_count)

    def forward_row(step, row):
        pre = jnp.dot(forward_ref[...], window(step, row), preferred_element_type=jnp.float32)
        in_gate = logistic(pre[:width])
        forget_gate = logistic(pre[width : 2 * width] + 1.0)
        out_gate = logistic(pre[2 * width : 3 * width])
        cand = jnp.tanh(pre[3 * width :])
        new_cell = forget_gate * cells[step, row] + in_gate * cand
        squash = jnp.tanh(new_cell)
        acts[step, row, :width] = in_gate
        acts[step, row, width : 2 * width] = forget_gate
        acts[step, row, 2 * width : 3 * width] = out_gate
        acts[step, row, 3 * width :] = cand
        squashes[step, row] = squash
        if step < steps - 1:
            cells[step + 1, row] = new_cell
            set_field(step + 1, row + 1, in_width, (out_gate * squash).astype(jnp.bfloat16))

    def for_rows(low, high, body):
        def run(row, _):
            body(row)
            return 0

        lax.fori_loop(low, high, run, 0)

    def build_weights():
        flat = jnp.concatenate(
            [shards[slot].astype(jnp.float32) for slot in shard_slots(depth)], axis=0
        )
        size = gates // 2
        half = lax.broadcasted_iota(jnp.int32, (size, 128), 1) < channels
        for pair in range(5):
            near = flat[2 * pair * size : (2 * pair + 1) * size]
            far = flat[(2 * pair + 1) * size : (2 * pair + 2) * size] if pair < 4 else near
            kernel_acc[pair, pl.ds(0, size, stride=2), :] = jnp.where(
                half, near, pltpu.roll(far, 64, 1)
            )
            kernel_acc[pair, pl.ds(1, size, stride=2), :] = jnp.where(
                half, pltpu.roll(near, 64, 1), far
            )
        for pair in range(5):
            mixed = kernel_acc[pair]
            flipped = mixed.T
            for tap in range(2 * pair, min(2 * pair + 2, 9)):
                low = (tap - 2 * pair) * channels
                row_tap, col_tap = tap // 3, tap % 3
                backward_ref[
                    col_tap * channels : (col_tap + 1) * channels,
                    (2 - row_tap) * gates : (3 - row_tap) * gates,
                ] = flipped[low : low + channels].astype(jnp.bfloat16)
            lanes = min(128, 9 * channels - pair * 128)
            forward_ref[:, pair * 128 : pair * 128 + lanes] = mixed[:, :lanes].astype(jnp.bfloat16)

    send_both(field_copy, 0)
    if depth:
        for stage in range(3):
            for copy in gathers[stage]:
                copy.wait()
            if stage < 2:
                for copy in gathers[stage + 1]:
                    copy.start()
        build_weights()
    for step in range(steps):
        if step:
            send_both(field_copy, step)
        for_rows(1, row_count - 1, functools.partial(forward_row, step))
        take_fields(step)
        forward_row(step, 0)
        forward_row(step, row_count - 1)

    def gate_row(step, row):
        in_gate = acts[step, row, :width]
        forget_gate = acts[step, row, width : 2 * width]
        out_gate = acts[step, row, 2 * width : 3 * width]
        cand = acts[step, row, 3 * width :]
        squash = squashes[step, row]
        hid_grad = cot_ref[step, row].astype(jnp.float32)
        if step < steps - 1:
            hid_grad = hid_grad + carry_h_ref[row]
        cell_grad = hid_grad * out_gate * (1.0 - squash * squash)
        if step < steps - 1:
            cell_grad = cell_grad + carry_c_ref[row]
        parts = (
            cell_grad * cand * in_gate * (1.0 - in_gate),
            cell_grad * cells[step, row] * forget_gate * (1.0 - forget_gate),
            hid_grad * squash * out_gate * (1.0 - out_gate),
            cell_grad * in_gate * (1.0 - cand * cand),
        )
        for index, part in enumerate(parts):
            grads[step, row + 1, index * width : (index + 1) * width] = part.astype(jnp.bfloat16)
        carry_c_ref[row] = cell_grad * forget_gate

    def back_row(step, row):
        stack = grads[step, pl.ds(row, 3)].reshape(3 * gates, col_count)
        out = jnp.dot(backward_ref[...], stack, preferred_element_type=jnp.float32)
        summed = (
            pltpu.roll(out[:channels], col_count - 1, 1) * has_right
            + out[channels : 2 * channels]
            + pltpu.roll(out[2 * channels :], 1, 1) * has_left
        )
        if step < steps - 1:
            input_acc[row] = input_acc[row] + summed[:in_width]
        else:
            input_acc[row] = summed[:in_width]
        carry_h_ref[row] = summed[in_width:]

    def kernel_rows(step, row):
        total = None
        for part in range(2):
            term = lax.dot_general(
                grads[step, row + part + 1],
                window(step, row + part),
                (((1,), (1,)), ((), ())),
                preferred_element_type=jnp.float32,
            )
            total = term if total is None else total + term
        for block in range(kernel_acc.shape[0]):
            part = total[:, block * 128 : (block + 1) * 128]
            lanes = part.shape[1]
            kernel_acc[block, :, :lanes] = kernel_acc[block, :, :lanes] + part

    kernel_acc[...] = jnp.zeros(kernel_acc.shape, jnp.float32)
    for step in reversed(range(steps)):
        gate_row(step, 0)
        gate_row(step, row_count - 1)
        send_both(grad_copy, step)
        for_rows(1, row_count - 1, functools.partial(gate_row, step))
        for_rows(1, row_count - 1, functools.partial(back_row, step))
        for_rows(0, row_count // 2, lambda pair: kernel_rows(step, 2 * pair))
        take_grads(step)
        back_row(step, 0)
        back_row(step, row_count - 1)

    def table_row(row, sums):
        grad = input_acc[row]
        return tuple(total + grad * mask for total, mask in zip(sums, masks(row)))

    zero = jnp.zeros((in_width, col_count), jnp.float32)
    sums = lax.fori_loop(0, row_count, table_row, (zero, zero, zero))
    columns = lax.broadcasted_iota(jnp.int32, (128, 128), 1)
    table = jnp.zeros((128, 128), jnp.float32)
    for index, total in enumerate(sums):
        column = jnp.sum(total, axis=1, keepdims=True)
        column = jnp.concatenate([column, jnp.zeros((128 - in_width, 1), jnp.float32)], axis=0)
        table = jnp.where(columns == index, column, table)
    flipped = table.T

    if not depth:
        for block in range(kernel_acc.shape[0]):
            lanes = min(128, 9 * channels - block * 128)
            kernel_ref[:, block * 128 : block * 128 + lanes] = kernel_acc[block, :, :lanes]
        table_ref[...] = flipped[:3, :in_width]
        return

    chunk_rows = shard_ref.shape[0]
    half = columns[: gates // 2] < channels
    lines = []
    for pair in range(5):
        even = kernel_acc[pair, pl.ds(0, gates // 2, stride=2), :]
        odd = kernel_acc[pair, pl.ds(1, gates // 2, stride=2), :]
        lines.append(jnp.where(half, even, pltpu.roll(odd, 64, 1)))
        if pair < 4:
            lines.append(jnp.where(half, pltpu.roll(even, 64, 1), odd))
    flat = jnp.concatenate(lines, axis=0)
    rest = chunks.shape[3] - chunk_rows - 3
    for index, slot in enumerate(shard_slots(depth)):
        part = flat[index * chunk_rows : (index + 1) * chunk_rows]
        pieces = [part, flipped[:3]]
        if rest:
            pieces.append(jnp.zeros((rest, 128), jnp.float32))
        chunks[slot] = jnp.concatenate(pieces, axis=0)

    copy = push(chunks.at[1 - core_me], core_land, core_scatter, 0, groups.core_peer())
    copy.start()
    copy.wait()
    chunks[core_me] = chunks[core_me] + core_land[...]
    copies = []
    for step in range(1, 4):
        plane, peer = groups.plane_peer(step)
        copies.append(
            push(chunks.at[core_me, plane], plane_land.at[plane_me], plane_scatter, step, peer)
        )
        copies[-1].start()
    plane_land[plane_me] = chunks[core_me, plane_me]
    for copy in copies:
        copy.wait()
    z_sum[...] = (plane_land[0] + plane_land[1]) + (plane_land[2] + plane_land[3])
    copies = []
    for step in range(1, depth):
        z, peer = groups.z_peer(step)
        copies.append(push(z_sum.at[z], z_land.at[z_me], z_scatter, step, peer))
        copies[-1].start()
    z_land[z_me] = z_sum[z_me]
    for copy in copies:
        copy.wait()
    total = z_land[0]
    for index in range(1, depth):
        total = total + z_land[index]
    total = total * scale
    kernel_ref[...] = total[:chunk_rows]
    table_ref[...] = total[chunk_rows : chunk_rows + 3, :in_width]


def per_device(
    maze_walls, goal_cell, start_hidden, start_cell, cotangent, gate_weights, embed_table
):
    rows = lax.axis_size("rows")
    mazes = lax.axis_size("maze")
    count = rows * mazes
    row_count = maze_walls.shape[1]
    col_count = maze_walls.shape[2]
    width = start_hidden.shape[1]
    in_width = embed_table.shape[1]
    channels = in_width + width
    gates = 4 * width
    steps = cotangent.shape[1]
    size = gate_weights.shape[0]
    hidden = start_hidden[0].transpose(1, 0, 2)
    cell = start_cell[0].transpose(1, 0, 2)
    cot = cotangent[0].transpose(0, 2, 1, 3)
    scale = 1.0 / math.sqrt(count * row_count * col_count * steps)

    direct = size % 128 == 0 and mazes == 2 and rows % 4 == 0 and channels == 64 and gates == 128
    depth = rows // 4 if direct else 0
    height = size // 128
    if direct:
        weights = [gate_weights.reshape(height, 128)]
        kernel_shape = (height, 128)
    else:
        gathered = lax.all_gather(gate_weights, ("rows", "maze"), axis=0, tiled=True)
        kernel = gathered.reshape(3, 3, gates, channels)
        weights = [
            kernel.transpose(2, 0, 1, 3).reshape(gates, 9 * channels),
            kernel[::-1].transpose(1, 3, 0, 2).reshape(3 * channels, 3 * gates),
        ]
        kernel_shape = (gates, 9 * channels)
    f32 = jnp.float32
    bf16 = jnp.bfloat16
    direct_scratch = []
    if direct:
        tall = -(-(height + 3) // 8) * 8
        direct_scratch = [
            pltpu.VMEM((gates, 9 * channels), bf16),
            pltpu.VMEM((3 * channels, 3 * gates), bf16),
            pltpu.VMEM((2, 4, depth, height, 128), bf16),
            pltpu.VMEM((2, 4, depth, tall, 128), f32),
            pltpu.VMEM((4, depth, tall, 128), f32),
            pltpu.VMEM((4, depth, tall, 128), f32),
            pltpu.VMEM((depth, tall, 128), f32),
            pltpu.VMEM((depth, tall, 128), f32),
        ] + [
            pltpu.SemaphoreType.DMA((2, slots)) for slots in (depth, 4, 1, 1, 4, depth)
        ]
    grad_kernel, table, carry_h, carry_c = pl.pallas_call(
        functools.partial(main_kernel, depth, scale),
        out_shape=(
            jax.ShapeDtypeStruct(kernel_shape, f32),
            jax.ShapeDtypeStruct((3, in_width), f32),
            jax.ShapeDtypeStruct((row_count, width, col_count), f32),
            jax.ShapeDtypeStruct((row_count, width, col_count), f32),
        ),
        in_specs=[SMEM] + [VMEM] * (5 + len(weights)),
        out_specs=(VMEM, VMEM, VMEM, VMEM),
        scratch_shapes=[
            pltpu.VMEM((steps, row_count + 2, 3 * channels, col_count), bf16),
            pltpu.VMEM((steps, row_count + 2, gates, col_count), bf16),
            pltpu.VMEM((steps, row_count, width, col_count), f32),
            pltpu.VMEM((steps, row_count, gates, col_count), f32),
            pltpu.VMEM((steps, row_count, width, col_count), f32),
            pltpu.VMEM((row_count, in_width, col_count), f32),
            pltpu.VMEM((-(-9 * channels // 128), gates, 128), f32),
            pltpu.VMEM((steps, 2, channels, col_count), bf16),
            pltpu.VMEM((steps, 2, gates, col_count), bf16),
            pltpu.SemaphoreType.DMA((steps, 2)),
            pltpu.SemaphoreType.DMA((steps, 2)),
            pltpu.SemaphoreType.DMA((steps, 2)),
            pltpu.SemaphoreType.DMA((steps, 2)),
        ]
        + direct_scratch,
        compiler_params=pltpu.CompilerParams(
            collective_id=0, has_side_effects=True, vmem_limit_bytes=48 * 1024 * 1024
        ),
    )(
        goal_cell,
        maze_walls[0],
        embed_table.T,
        hidden,
        cell,
        cot,
        *weights,
    )
    if direct:
        grad_weights = grad_kernel.reshape(-1)
        grad_table = table
    else:
        ordered = grad_kernel.reshape(gates, 9, channels).transpose(1, 0, 2).reshape(-1)
        grad_weights = scale * lax.psum_scatter(
            ordered, ("rows", "maze"), scatter_dimension=0, tiled=True
        )
        grad_table = scale * lax.psum(table, ("rows", "maze"))
    return (
        grad_weights,
        grad_table,
        carry_h.transpose(1, 0, 2)[None],
        carry_c.transpose(1, 0, 2)[None],
    )


def solution(mesh):
    return jax.shard_map(
        per_device,
        mesh=mesh,
        in_specs=(
            P("maze", "rows", None),
            P("maze", None),
            P("maze", None, "rows", None),
            P("maze", None, "rows", None),
            P("maze", None, None, "rows", None),
            P(("rows", "maze")),
            P(),
        ),
        out_specs=(
            P(("rows", "maze")),
            P(),
            P("maze", None, "rows", None),
            P("maze", None, "rows", None),
        ),
        check_vma=False,
    )
```

```python
import functools
import math

import jax
import jax.numpy as jnp
from jax import lax
from jax.experimental import pallas as pl
from jax.experimental.pallas import tpu as pltpu
from jax.sharding import PartitionSpec as P

goal_reach = 64.0
MESH = pl.DeviceIdType.MESH
VMEM = pl.BlockSpec(memory_space=pltpu.VMEM)
SMEM = pl.BlockSpec(memory_space=pltpu.SMEM)


class Groups:
    def __init__(self, depth):
        rows = lax.axis_index("rows")
        self.depth = depth
        self.maze = lax.axis_index("maze")
        self.core = lax.rem(rows, 2)
        self.z = lax.div(rows, 4)
        self.y = lax.rem(lax.div(rows, 2), 2)
        self.plane = self.y * 2 + self.maze

    def device(self, z, plane, core):
        return {"rows": z * 4 + lax.div(plane, 2) * 2 + core, "maze": lax.rem(plane, 2)}

    def z_peer(self, step):
        z = lax.rem(self.z + step, self.depth)
        return z, self.device(z, self.plane, self.core)

    def plane_peer(self, step):
        plane = lax.rem(self.plane + step, 4)
        return plane, self.device(self.z, plane, self.core)

    def core_peer(self):
        return self.device(self.z, self.plane, 1 - self.core)

    def peers(self):
        found = [self.z_peer(step)[1] for step in range(1, self.depth)]
        found += [self.plane_peer(step)[1] for step in range(1, 4)]
        return found + [self.core_peer()]


def shard_slots(depth):
    return [
        (core, 2 * y + maze, z)
        for z in range(depth)
        for y in range(2)
        for core in range(2)
        for maze in range(2)
    ]


def push(src, dst, sems, slot, device):
    return pltpu.make_async_remote_copy(
        src_ref=src,
        dst_ref=dst,
        send_sem=sems.at[0, slot],
        recv_sem=sems.at[1, slot],
        device_id=device,
        device_id_type=MESH,
    )


def logistic(x):
    return 0.5 * jnp.tanh(0.5 * x) + 0.5


def main_kernel(
    depth,
    scale,
    goal_ref,
    walls_ref,
    embed_ref,
    hidden_ref,
    cell_ref,
    cot_ref,
    *refs,
):
    if depth:
        shard_ref, *refs = refs
    else:
        forward_ref, backward_ref, *refs = refs
    kernel_ref, table_ref, carry_h_ref, carry_c_ref, *refs = refs
    if depth:
        refs, extra = refs[:-17], refs[-17:]
        forward_ref, backward_ref, shards, chunks = extra[:4]
        core_land, plane_land, z_sum, z_land = extra[4:8]
        table_part, table_land = extra[8:10]
        z_gather, plane_gather, core_gather = extra[10:13]
        core_scatter, plane_scatter, z_scatter, table_sems = extra[13:]
    (
    fields,
    grads,
    cells,
    acts,
    squashes,
    input_acc,
    kernel_acc,
    field_land,
    grad_land,
    field_send,
    field_recv,
    grad_send,
    grad_recv,
    ) = refs
    row_count, width, col_count = hidden_ref.shape
    in_width = embed_ref.shape[0]
    channels = in_width + width
    gates = 4 * width
    steps = cot_ref.shape[0]
    me = lax.axis_index("rows")
    ends = lax.axis_size("rows") - 1
    lane = lax.broadcasted_iota(jnp.int32, (1, col_count), 1)
    has_left = (lane > 0).astype(jnp.float32)
    has_right = (lane < col_count - 1).astype(jnp.float32)

    barrier = pltpu.get_barrier_semaphore()

    @pl.when(me > 0)
    def _():
        pl.semaphore_signal(barrier, inc=1, device_id={"rows": me - 1}, device_id_type=MESH)

    @pl.when(me < ends)
    def _():
        pl.semaphore_signal(barrier, inc=1, device_id={"rows": me + 1}, device_id_type=MESH)

    group_peers = 0
    if depth:
        groups = Groups(depth)
        z_me, plane_me, core_me = groups.z, groups.plane, groups.core
        for peer in groups.peers():
            pl.semaphore_signal(barrier, inc=1, device_id=peer, device_id_type=MESH)
            group_peers += 1
        shards[core_me, plane_me, z_me] = shard_ref[...]
    middle = jnp.logical_and(me > 0, me < ends)

    @pl.when(middle)
    def _():
        pl.semaphore_wait(barrier, group_peers + 2)

    @pl.when(jnp.logical_not(middle))
    def _():
        pl.semaphore_wait(barrier, group_peers + 1)

    gathers = ([], [], [])
    if depth:
        for step in range(1, depth):
            part = shards.at[core_me, plane_me, z_me]
            gathers[0].append(push(part, part, z_gather, step, groups.z_peer(step)[1]))
        for step in range(1, 4):
            part = shards.at[core_me, plane_me]
            gathers[1].append(push(part, part, plane_gather, step, groups.plane_peer(step)[1]))
        part = shards.at[core_me]
        gathers[2].append(push(part, part, core_gather, 0, groups.core_peer()))
        for copy in gathers[0]:
            copy.start()

    def masks(row):
        wall = (walls_ref[pl.ds(row, 1), :] == 1).astype(jnp.float32)
        row_dist = jnp.abs(me * row_count + row - goal_ref[0, 0])
        dist = (row_dist + jnp.abs(lane - goal_ref[0, 1])).astype(jnp.float32)
        return 1.0 - wall, wall, jnp.exp(-dist / goal_reach)

    def set_field(step, row, low, values):
        high = low + values.shape[0]
        wide = values.astype(jnp.float32)
        fields[step, row, low:high] = (pltpu.roll(wide, 1, 1) * has_left).astype(jnp.bfloat16)
        fields[step, row, channels + low : channels + high] = values
        fields[step, row, 2 * channels + low : 2 * channels + high] = (
            pltpu.roll(wide, col_count - 1, 1) * has_right
        ).astype(jnp.bfloat16)

    def share_inputs(step, row):
        for tap in range(3):
            part = slice(tap * channels, tap * channels + in_width)
            fields[step, row, part] = fields[0, row, part]

    def first_row(row, _):
        open_mask, wall_mask, bump = masks(row)
        values = (
            embed_ref[:, 0:1] * open_mask + embed_ref[:, 1:2] * wall_mask + embed_ref[:, 2:3] * bump
        ).astype(jnp.bfloat16)
        set_field(0, row + 1, 0, values)
        set_field(0, row + 1, in_width, hidden_ref[row])
        for step in range(1, steps):
            share_inputs(step, row + 1)
        cells[0, row] = cell_ref[row]
        return 0

    lax.fori_loop(0, row_count, first_row, 0, unroll=True)


    def field_copy(step, side):
        low = channels if step == 0 else channels + in_width
        size = 2 * channels - low
        row = 1 if side == 0 else row_count
        return pltpu.make_async_remote_copy(
            src_ref=fields.at[step, row, pl.ds(low, size)],
            dst_ref=field_land.at[step, 1 - side, pl.ds(low - channels, size)],
            send_sem=field_send.at[step, side],
            recv_sem=field_recv.at[step, 1 - side],
            device_id={"rows": me - 1 if side == 0 else me + 1},
            device_id_type=MESH,
        )

    def grad_copy(step, side):
        row = 1 if side == 0 else row_count
        return pltpu.make_async_remote_copy(
            src_ref=grads.at[step, row],
            dst_ref=grad_land.at[step, 1 - side],
            send_sem=grad_send.at[step, side],
            recv_sem=grad_recv.at[step, 1 - side],
            device_id={"rows": me - 1 if side == 0 else me + 1},
            device_id_type=MESH,
        )

    def send_both(copy, step):
        @pl.when(me > 0)
        def _():
            copy(step, 0).start()

        @pl.when(me < ends)
        def _():
            copy(step, 1).start()

    def take_fields(step):
        low = 0 if step == 0 else in_width
        for side, row, there in ((0, 0, me > 0), (1, row_count + 1, me < ends)):

            @pl.when(there)
            def _():
                field_copy(step, side).wait_send()
                field_copy(step, 1 - side).wait_recv()
                if step:
                    share_inputs(step, row)
                set_field(step, row, low, field_land[step, side, low:channels])

            @pl.when(jnp.logical_not(there))
            def _():
                fields[step, row] = jnp.zeros((3 * channels, col_count), jnp.bfloat16)

    def take_grads(step):
        for side, row, there in ((0, 0, me > 0), (1, row_count + 1, me < ends)):

            @pl.when(there)
            def _():
                grad_copy(step, side).wait_send()
                grad_copy(step, 1 - side).wait_recv()
                grads[step, row] = grad_land[step, side]

            @pl.when(jnp.logical_not(there))
            def _():
                grads[step, row] = jnp.zeros((gates, col_count), jnp.bfloat16)

    def window(step, row):
        return fields[step, pl.ds(row, 3)].reshape(9 * channels, col_count)

    def forward_row(step, row):
        pre = jnp.dot(forward_ref[...], window(step, row), preferred_element_type=jnp.float32)
        in_gate = logistic(pre[:width])
        forget_gate = logistic(pre[width : 2 * width] + 1.0)
        out_gate = logistic(pre[2 * width : 3 * width])
        cand = jnp.tanh(pre[3 * width :])
        new_cell = forget_gate * cells[step, row] + in_gate * cand
        squash = jnp.tanh(new_cell)
        acts[step, row, :width] = in_gate
        acts[step, row, width : 2 * width] = forget_gate
        acts[step, row, 2 * width : 3 * width] = out_gate
        acts[step, row, 3 * width :] = cand
        squashes[step, row] = squash
        if step < steps - 1:
            cells[step + 1, row] = new_cell
            set_field(step + 1, row + 1, in_width, (out_gate * squash).astype(jnp.bfloat16))

    def for_rows(low, high, body):
        def run(row, _):
            body(row)
            return 0

        lax.fori_loop(low, high, run, 0, unroll=True)

    def build_weights():
        flat = jnp.concatenate(
            [shards[slot].astype(jnp.float32) for slot in shard_slots(depth)], axis=0
        )
        size = gates // 2
        half = lax.broadcasted_iota(jnp.int32, (size, 128), 1) < channels
        for pair in range(5):
            near = flat[2 * pair * size : (2 * pair + 1) * size]
            far = flat[(2 * pair + 1) * size : (2 * pair + 2) * size] if pair < 4 else near
            kernel_acc[pair, pl.ds(0, size, stride=2), :] = jnp.where(
                half, near, pltpu.roll(far, 64, 1)
            )
            kernel_acc[pair, pl.ds(1, size, stride=2), :] = jnp.where(
                half, pltpu.roll(near, 64, 1), far
            )
        for pair in range(5):
            mixed = kernel_acc[pair]
            flipped = mixed.T
            for tap in range(2 * pair, min(2 * pair + 2, 9)):
                low = (tap - 2 * pair) * channels
                row_tap, col_tap = tap // 3, tap % 3
                backward_ref[
                    col_tap * channels : (col_tap + 1) * channels,
                    (2 - row_tap) * gates : (3 - row_tap) * gates,
                ] = flipped[low : low + channels].astype(jnp.bfloat16)
            lanes = min(128, 9 * channels - pair * 128)
            forward_ref[:, pair * 128 : pair * 128 + lanes] = mixed[:, :lanes].astype(jnp.bfloat16)

    send_both(field_copy, 0)
    if depth:
        for stage in range(3):
            for copy in gathers[stage]:
                copy.wait()
            if stage < 2:
                for copy in gathers[stage + 1]:
                    copy.start()
        build_weights()
    for step in range(steps):
        if step:
            send_both(field_copy, step)
        for_rows(1, row_count - 1, functools.partial(forward_row, step))
        take_fields(step)
        forward_row(step, 0)
        forward_row(step, row_count - 1)

    def gate_row(step, row):
        in_gate = acts[step, row, :width]
        forget_gate = acts[step, row, width : 2 * width]
        out_gate = acts[step, row, 2 * width : 3 * width]
        cand = acts[step, row, 3 * width :]
        squash = squashes[step, row]
        hid_grad = cot_ref[step, row].astype(jnp.float32)
        if step < steps - 1:
            hid_grad = hid_grad + carry_h_ref[row]
        cell_grad = hid_grad * out_gate * (1.0 - squash * squash)
        if step < steps - 1:
            cell_grad = cell_grad + carry_c_ref[row]
        parts = (
            cell_grad * cand * in_gate * (1.0 - in_gate),
            cell_grad * cells[step, row] * forget_gate * (1.0 - forget_gate),
            hid_grad * squash * out_gate * (1.0 - out_gate),
            cell_grad * in_gate * (1.0 - cand * cand),
        )
        for index, part in enumerate(parts):
            grads[step, row + 1, index * width : (index + 1) * width] = part.astype(jnp.bfloat16)
        carry_c_ref[row] = cell_grad * forget_gate

    def back_row(step, row):
        stack = grads[step, pl.ds(row, 3)].reshape(3 * gates, col_count)
        out = jnp.dot(backward_ref[...], stack, preferred_element_type=jnp.float32)
        summed = (
            pltpu.roll(out[:channels], col_count - 1, 1) * has_right
            + out[channels : 2 * channels]
            + pltpu.roll(out[2 * channels :], 1, 1) * has_left
        )
        if step < steps - 1:
            input_acc[row] = input_acc[row] + summed[:in_width]
        else:
            input_acc[row] = summed[:in_width]
        carry_h_ref[row] = summed[in_width:]

    def kernel_rows(step, row):
        total = None
        for part in range(2):
            term = lax.dot_general(
                grads[step, row + part + 1],
                window(step, row + part),
                (((1,), (1,)), ((), ())),
                preferred_element_type=jnp.float32,
            )
            total = term if total is None else total + term
        for block in range(kernel_acc.shape[0]):
            part = total[:, block * 128 : (block + 1) * 128]
            lanes = part.shape[1]
            kernel_acc[block, :, :lanes] = kernel_acc[block, :, :lanes] + part

    def start_scatter():
        chunk_rows = shard_ref.shape[0]
        half = lax.broadcasted_iota(jnp.int32, (gates // 2, 128), 1) < channels
        lines = []
        for pair in range(5):
            even = kernel_acc[pair, pl.ds(0, gates // 2, stride=2), :]
            odd = kernel_acc[pair, pl.ds(1, gates // 2, stride=2), :]
            lines.append(jnp.where(half, even, pltpu.roll(odd, 64, 1)))
            if pair < 4:
                lines.append(jnp.where(half, pltpu.roll(even, 64, 1), odd))
        flat = jnp.concatenate(lines, axis=0)
        rest = chunks.shape[3] - chunk_rows
        for index, slot in enumerate(shard_slots(depth)):
            part = flat[index * chunk_rows : (index + 1) * chunk_rows]
            chunks[slot] = jnp.concatenate([part, jnp.zeros((rest, 128), jnp.float32)], axis=0)
        copy = push(chunks.at[1 - core_me], core_land, core_scatter, 0, groups.core_peer())
        copy.start()
        return copy

    kernel_acc[...] = jnp.zeros(kernel_acc.shape, jnp.float32)
    for step in reversed(range(steps)):
        gate_row(step, 0)
        gate_row(step, row_count - 1)
        send_both(grad_copy, step)
        for_rows(1, row_count - 1, functools.partial(gate_row, step))
        if step:
            for_rows(1, row_count - 1, functools.partial(back_row, step))
            for_rows(0, row_count // 2, lambda pair: kernel_rows(step, 2 * pair))
        else:
            for_rows(0, row_count // 2, lambda pair: kernel_rows(step, 2 * pair))
            core_copy = start_scatter() if depth else None
            for_rows(1, row_count - 1, functools.partial(back_row, step))
        take_grads(step)
        back_row(step, 0)
        back_row(step, row_count - 1)

    def table_row(row, sums):
        grad = input_acc[row]
        return tuple(total + grad * mask for total, mask in zip(sums, masks(row)))

    zero = jnp.zeros((in_width, col_count), jnp.float32)
    sums = lax.fori_loop(0, row_count, table_row, (zero, zero, zero))
    columns = lax.broadcasted_iota(jnp.int32, (128, 128), 1)
    table = jnp.zeros((128, 128), jnp.float32)
    for index, total in enumerate(sums):
        column = jnp.sum(total, axis=1, keepdims=True)
        column = jnp.concatenate([column, jnp.zeros((128 - in_width, 1), jnp.float32)], axis=0)
        table = jnp.where(columns == index, column, table)
    flipped = table.T

    if not depth:
        for block in range(kernel_acc.shape[0]):
            lanes = min(128, 9 * channels - block * 128)
            kernel_ref[:, block * 128 : block * 128 + lanes] = kernel_acc[block, :, :lanes]
        table_ref[...] = flipped[:3, :in_width]
        return

    chunk_rows = shard_ref.shape[0]
    table_part[...] = flipped[:8]
    table_copy = push(table_part, table_land, table_sems, 0, groups.core_peer())
    table_copy.start()
    core_copy.wait()
    table_copy.wait()
    lines = lax.broadcasted_iota(jnp.int32, (8, 128), 0)
    pair_table = jnp.where(lines < 3, table_part[...] + table_land[...], 0.0)
    pad = chunks.shape[3] - chunk_rows - 3
    placed = jnp.concatenate(
        [jnp.zeros((chunk_rows, 128), jnp.float32), pair_table[: 3 + pad]], axis=0
    )
    chunks[core_me] = chunks[core_me] + core_land[...] + placed
    copies = []
    for step in range(1, 4):
        plane, peer = groups.plane_peer(step)
        copies.append(
            push(chunks.at[core_me, plane], plane_land.at[plane_me], plane_scatter, step, peer)
        )
        copies[-1].start()
    plane_land[plane_me] = chunks[core_me, plane_me]
    for copy in copies:
        copy.wait()
    z_sum[...] = (plane_land[0] + plane_land[1]) + (plane_land[2] + plane_land[3])
    copies = []
    for step in range(1, depth):
        z, peer = groups.z_peer(step)
        copies.append(push(z_sum.at[z], z_land.at[z_me], z_scatter, step, peer))
        copies[-1].start()
    z_land[z_me] = z_sum[z_me]
    for copy in copies:
        copy.wait()
    total = z_land[0]
    for index in range(1, depth):
        total = total + z_land[index]
    total = total * scale
    kernel_ref[...] = total[:chunk_rows]
    table_ref[...] = total[chunk_rows : chunk_rows + 3, :in_width]


def per_device(
    maze_walls, goal_cell, start_hidden, start_cell, cotangent, gate_weights, embed_table
):
    rows = lax.axis_size("rows")
    mazes = lax.axis_size("maze")
    count = rows * mazes
    row_count = maze_walls.shape[1]
    col_count = maze_walls.shape[2]
    width = start_hidden.shape[1]
    in_width = embed_table.shape[1]
    channels = in_width + width
    gates = 4 * width
    steps = cotangent.shape[1]
    size = gate_weights.shape[0]
    hidden = start_hidden[0].transpose(1, 0, 2)
    cell = start_cell[0].transpose(1, 0, 2)
    cot = cotangent[0].transpose(0, 2, 1, 3)
    scale = 1.0 / math.sqrt(count * row_count * col_count * steps)

    direct = size % 128 == 0 and mazes == 2 and rows % 4 == 0 and channels == 64 and gates == 128
    depth = rows // 4 if direct else 0
    height = size // 128
    if direct:
        weights = [gate_weights.reshape(height, 128)]
        kernel_shape = (height, 128)
    else:
        gathered = lax.all_gather(gate_weights, ("rows", "maze"), axis=0, tiled=True)
        kernel = gathered.reshape(3, 3, gates, channels)
        weights = [
            kernel.transpose(2, 0, 1, 3).reshape(gates, 9 * channels),
            kernel[::-1].transpose(1, 3, 0, 2).reshape(3 * channels, 3 * gates),
        ]
        kernel_shape = (gates, 9 * channels)
    f32 = jnp.float32
    bf16 = jnp.bfloat16
    direct_scratch = []
    if direct:
        tall = -(-(height + 3) // 8) * 8
        direct_scratch = [
            pltpu.VMEM((gates, 9 * channels), bf16),
            pltpu.VMEM((3 * channels, 3 * gates), bf16),
            pltpu.VMEM((2, 4, depth, height, 128), bf16),
            pltpu.VMEM((2, 4, depth, tall, 128), f32),
            pltpu.VMEM((4, depth, tall, 128), f32),
            pltpu.VMEM((4, depth, tall, 128), f32),
            pltpu.VMEM((depth, tall, 128), f32),
            pltpu.VMEM((depth, tall, 128), f32),
            pltpu.VMEM((8, 128), f32),
            pltpu.VMEM((8, 128), f32),
        ] + [
            pltpu.SemaphoreType.DMA((2, slots)) for slots in (depth, 4, 1, 1, 4, depth, 1)
        ]
    grad_kernel, table, carry_h, carry_c = pl.pallas_call(
        functools.partial(main_kernel, depth, scale),
        out_shape=(
            jax.ShapeDtypeStruct(kernel_shape, f32),
            jax.ShapeDtypeStruct((3, in_width), f32),
            jax.ShapeDtypeStruct((row_count, width, col_count), f32),
            jax.ShapeDtypeStruct((row_count, width, col_count), f32),
        ),
        in_specs=[SMEM] + [VMEM] * (5 + len(weights)),
        out_specs=(VMEM, VMEM, VMEM, VMEM),
        scratch_shapes=[
            pltpu.VMEM((steps, row_count + 2, 3 * channels, col_count), bf16),
            pltpu.VMEM((steps, row_count + 2, gates, col_count), bf16),
            pltpu.VMEM((steps, row_count, width, col_count), f32),
            pltpu.VMEM((steps, row_count, gates, col_count), f32),
            pltpu.VMEM((steps, row_count, width, col_count), f32),
            pltpu.VMEM((row_count, in_width, col_count), f32),
            pltpu.VMEM((-(-9 * channels // 128), gates, 128), f32),
            pltpu.VMEM((steps, 2, channels, col_count), bf16),
            pltpu.VMEM((steps, 2, gates, col_count), bf16),
            pltpu.SemaphoreType.DMA((steps, 2)),
            pltpu.SemaphoreType.DMA((steps, 2)),
            pltpu.SemaphoreType.DMA((steps, 2)),
            pltpu.SemaphoreType.DMA((steps, 2)),
        ]
        + direct_scratch,
        compiler_params=pltpu.CompilerParams(
            collective_id=0, has_side_effects=True, vmem_limit_bytes=48 * 1024 * 1024
        ),
    )(
        goal_cell,
        maze_walls[0],
        embed_table.T,
        hidden,
        cell,
        cot,
        *weights,
    )
    if direct:
        grad_weights = grad_kernel.reshape(-1)
        grad_table = table
    else:
        ordered = grad_kernel.reshape(gates, 9, channels).transpose(1, 0, 2).reshape(-1)
        grad_weights = scale * lax.psum_scatter(
            ordered, ("rows", "maze"), scatter_dimension=0, tiled=True
        )
        grad_table = scale * lax.psum(table, ("rows", "maze"))
    return (
        grad_weights,
        grad_table,
        carry_h.transpose(1, 0, 2)[None],
        carry_c.transpose(1, 0, 2)[None],
    )


def solution(mesh):
    return jax.shard_map(
        per_device,
        mesh=mesh,
        in_specs=(
            P("maze", "rows", None),
            P("maze", None),
            P("maze", None, "rows", None),
            P("maze", None, "rows", None),
            P("maze", None, None, "rows", None),
            P(("rows", "maze")),
            P(),
        ),
        out_specs=(
            P(("rows", "maze")),
            P(),
            P("maze", None, "rows", None),
            P("maze", None, "rows", None),
        ),
        check_vma=False,
    )
```
